512 devices in a mesh: table: 64 (over y, z), dp: 8 (over x, core).
Axes of the slice: x: 4, y: 4, z: 16, core: 2. Of those that a mesh axis runs over, the one named last changes fastest.
Arguments:
- table: bfloat16 [24576, 512], P('table'), may hold values from -6 to 6
- owner: int32 [512, 256, 1], P(('table', 'dp')), may hold values from 0 to 63; in each aligned block of 256 rows (0 to 255, 256 to 511, ..., all dimensions but the last counted through in order) at most 8 rows name the same one
- row_in_shard: int32 [512, 256], P(('table', 'dp')), may hold values from 0 to 383
- segment: int32 [512, 256], P(('table', 'dp')), may hold values from 0 to 3, never falling along the last dimension, each value on 1 to 128 neighbouring positions
- w_in: bfloat16 [512, 2048], replicated, may hold values from -0.25 to 0.25
- w_out: bfloat16 [512, 512], replicated, may hold values from -0.25 to 0.25
- cotangent: bfloat16 [512, 256, 512], P(('table', 'dp')), may hold values from -6 to 6
Outputs:
- layer_out: bfloat16 [512, 256, 512], P(('table', 'dp'))
- grad_table: float32 [24576, 512], P('table')
- grad_w_in: float32 [512, 2048], P(None, 'dp')
- grad_w_out: float32 [512, 512], P('dp')
The draws below stay inside these ranges and needn't reach their ends.
Inputs may be any that keep to these rules, and one draw needn't show every extreme that they name: `owner`: among one device's 256 positions no shard is named more than 8 times, a bound that some block reaches. `segment`: never falls along a buffer; each history has 1 to 128 positions and one has exactly 128.
All inputs are finite; a program needn't handle non-finite values.
Results may differ from the reference program's by a relative error of at most 0.019.
Values may be sent and summed in bfloat16 or wider, within the bound.
No kernel may reach another device: no remote copies, remote signals or barrier semaphores. Data moves between devices by JAX's collectives and lax.ppermute only.
A program may use at most 64 MiB of HBM per device.

```python
import math
import jax
import jax.numpy as jnp
import numpy as np
from jax import lax

D = 512
HEADS = 8
ROWS = 256
NSEG = 4
VOCAB_DEV = 384
MOST = 128
CAP = 8
GROUPS = 512
VOCAB = 24576
N_TABLE = 64


def plant(values, own_key, low, high):
    extent = values.shape
    place = [jax.random.randint(jax.random.fold_in(own_key, axis), (), 0, extent[axis]) for axis in range(len(extent))]
    values = values.at[tuple(place)].set(low)
    longest = extent.index(max(extent))
    place[longest] = (place[longest] + 1) % extent[longest]
    return values.at[tuple(place)].set(high)


def block_levels(rng, dims, shards, low, largest):
    def one(dim, blocks):
        steps = jax.random.uniform(jax.random.fold_in(jax.random.fold_in(rng, 6), dim), (blocks,), jnp.float32, low / len(shards), largest / len(shards))
        return jnp.repeat(jnp.exp(steps), dims[dim] // blocks).reshape((-1,) + (1,) * (len(dims) - dim - 1))

    gain = one(*shards[0])
    for cut in shards[1:]:
        gain = gain * one(*cut)
    return gain


def length_profile(amount, total, limit, skew):
    portions = [(1 << 20) // math.isqrt(standing ** skew) + 1 for standing in range(2, amount + 1)]
    rest, given = total - limit - (amount - 1), [1] * (amount - 1)
    while rest > 0:
        free = [i for i in range(amount - 1) if given[i] < limit]
        mass, remaining = sum([portions[i] for i in free]), rest
        for i in free:
            addition = min(limit - given[i], max(1, remaining * portions[i] // mass), rest)
            given[i] = given[i] + addition
            rest = rest - addition
    return np.array([limit] + given)


def uneven(key, count, total, most, slope):
    if count == 2:
        one = jax.random.randint(key, (), max(1, total - most), min(most, total - 1) + 1)
        return jnp.stack([one, total - one])
    sizes = jnp.asarray(length_profile(count, total, most, slope), jnp.int32)
    twos = (count - 1) // 2
    source_of, receiver = sizes[1:1 + 2 * twos:2], sizes[2:2 + 2 * twos:2]
    room = jnp.minimum(source_of - 1, most - receiver)
    passed = jax.random.randint(jax.random.fold_in(key, 1), (twos,), 0, 1 << 20) % (room + 1)
    sizes = sizes.at[1:1 + 2 * twos:2].set(source_of - passed).at[2:2 + 2 * twos:2].set(receiver + passed)
    return sizes[jax.random.permutation(jax.random.fold_in(key, 2), count)]


def shared_out(key, own, number, rows, count, top, most, lean):
    order = jax.random.permutation(key, count)
    packed, common = portions_of(count, rows * top, most, lean, True), portions_of(count, rows * top, most, lean, False)
    places = jnp.arange(count)

    def named(tallies, rotation):
        used = int((tallies > 0).sum())
        fixed = max(1, used // 4)
        moved = fixed + (places - fixed + rotation * (used - fixed)) % max(1, count - fixed)
        return jnp.zeros((count,), jnp.int32).at[order[jnp.where(places < fixed, places, moved)]].set(jnp.asarray(tallies, jnp.int32))

    tallies = jnp.where(number % 4 == 0, named(packed, number // 4), named(common, number - number // 4 - 1))
    mixed = jax.random.permutation(jax.random.fold_in(own, 3), count)
    giver, sink = mixed[0:count // 2 * 2:2], mixed[1:count // 2 * 2:2]
    slack = jnp.minimum(tallies[giver] - 1, most - tallies[sink]) // 2
    slack = jnp.where((giver == order[0]) | (sink == order[0]) | (tallies[sink] == 0), 0, jnp.maximum(slack, 0))
    moved = jax.random.randint(jax.random.fold_in(own, 4), (count // 2,), 0, 1 << 20) % (slack + 1)
    tallies = tallies.at[giver].add(-moved).at[sink].add(moved)
    members = jnp.searchsorted(jnp.cumsum(tallies), jnp.arange(rows * top), side="right").astype(jnp.int32)
    table = members.reshape(top, rows).T
    table = table[jax.random.permutation(jax.random.fold_in(own, 1), rows)]
    rotation = jax.random.randint(jax.random.fold_in(own, 2), (rows, 1), 0, top)
    return jnp.take_along_axis(table, (jnp.arange(top)[None, :] + rotation) % top, axis=1)


def portions_of(number_of, total, most, skew, full):
    weights = [(1 << 20) // math.isqrt(standing ** skew) + 1 for standing in range(1, number_of + 1)]
    largest = most if full else min(most, max(-(-total // number_of), total * weights[0] // sum(weights)))
    least = 1 if total - largest >= number_of - 1 else 0
    holding, surplus = [largest] + [least] * (number_of - 1), total - largest - least * (number_of - 1)
    while surplus > 0:
        free = [i for i in range(1, number_of) if holding[i] < largest] or [i for i in range(1, number_of) if holding[i] < most]
        pool, budget = sum([weights[i] for i in free]), surplus
        for i in free:
            more = min(most - holding[i], max(1, budget * weights[i] // pool), surplus)
            holding[i] = holding[i] + more
            surplus = surplus - more
    return np.array(holding)


def noise(rng, shape, deviation, limit, cuts=(), held_as=jnp.bfloat16):
    gain = block_levels(rng, shape, cuts, -0.22, 0.18) if cuts else 1.0
    drawn = jax.random.normal(rng, shape, jnp.float32) * deviation * gain
    return jnp.minimum(jnp.maximum(drawn, -limit), limit).astype(held_as)


def setup_inputs(seed: int = 0) -> dict:
    splits = jax.random.split(jax.random.key(seed), 8)
    table = noise(splits[0], (VOCAB, D), 1.0, 6.0, ((0, 64),))
    owner_keys = jax.random.split(jax.random.fold_in(splits[1], 1), GROUPS * ROWS // ROWS)
    owner_turns = jax.random.permutation(jax.random.fold_in(splits[1], 3), GROUPS * ROWS // ROWS)
    owner = jax.vmap(lambda own, number: shared_out(jax.random.fold_in(splits[1], 2), own, number, ROWS, N_TABLE, 1, CAP, 2))(owner_keys, owner_turns).reshape((GROUPS, ROWS, 1))
    row_in_shard = plant(jax.random.randint(splits[2], (GROUPS, ROWS), 0, VOCAB_DEV), jax.random.fold_in(splits[2], 1), 0, VOCAB_DEV - 1).astype(jnp.int32)
    segment = jax.vmap(lambda own: jnp.searchsorted(jnp.cumsum(uneven(own, NSEG, ROWS, MOST, 2)), jnp.arange(ROWS), side="right"))(jax.random.split(splits[3], GROUPS)).reshape((GROUPS, ROWS)).astype(jnp.int32)
    w_in = noise(splits[4], (D, 4 * D), D ** -0.5, 0.25)
    w_out = noise(splits[5], (D, D), D ** -0.5, 0.25)
    cotangent = noise(splits[6], (GROUPS, ROWS, D), 1.0, 6.0, ((0, 512),))
    return {"table": table, "owner": owner, "row_in_shard": row_in_shard, "segment": segment, "w_in": w_in, "w_out": w_out, "cotangent": cotangent}


EPS = 1e-05

def normalize(values):
    average = lax.optimization_barrier(jnp.mean(values, axis=-1, keepdims=True))
    centred = values - average
    spread = lax.optimization_barrier(jnp.mean(centred * centred, axis=-1, keepdims=True))
    return centred * lax.rsqrt(spread + EPS)

def hstu_layer(embedded, w_in, w_out, segment):
    row_count, width = embedded.shape
    head_size = width // HEADS
    normed = normalize(embedded.astype(jnp.float32)).astype(jnp.bfloat16)
    mixed_all = jax.nn.silu(jnp.dot(normed, w_in, preferred_element_type=jnp.float32)).astype(jnp.bfloat16)
    gate_part = mixed_all[:, :width]
    value_part = mixed_all[:, width:2 * width].reshape(row_count, HEADS, head_size)
    query_part = mixed_all[:, 2 * width:3 * width].reshape(row_count, HEADS, head_size)
    key_part = mixed_all[:, 3 * width:].reshape(row_count, HEADS, head_size)
    position = jnp.arange(row_count)
    allowed = (segment[:, None] == segment[None, :]) & (position[None, :] <= position[:, None])
    scores = jnp.einsum('qhd,khd->hqk', query_part.astype(jnp.float32), key_part.astype(jnp.float32)) * head_size ** (-0.5)
    weights = jnp.where(allowed[None], jax.nn.silu(scores), 0.0).astype(jnp.bfloat16)
    attended = jnp.einsum('hqk,khd->qhd', weights.astype(jnp.float32), value_part.astype(jnp.float32)).reshape(row_count, width)
    gated = (normalize(attended) * gate_part.astype(jnp.float32)).astype(jnp.bfloat16)
    result = embedded.astype(jnp.float32) + jnp.dot(gated, w_out, preferred_element_type=jnp.float32)
    return result.astype(jnp.bfloat16)

def reference(table, owner, row_in_shard, segment, w_in, w_out, cotangent):
    item_index = (owner[:, :, 0] * VOCAB_DEV + row_in_shard).astype(jnp.int32)
    embedded = jnp.take(table, item_index, axis=0)

    def per_group(carry, inputs):
        emb_rows, seg_rows, cot_rows = inputs

        def local_layer(emb_in, weight_in, weight_out):
            return hstu_layer(emb_in, weight_in, weight_out, seg_rows)
        layer_rows, pullback = jax.vjp(local_layer, emb_rows, w_in, w_out)
        d_emb, d_in, d_out = pullback(cot_rows)
        return ((carry[0] + d_in.astype(jnp.float32), carry[1] + d_out.astype(jnp.float32)), (layer_rows, d_emb))
    start = (jnp.zeros(w_in.shape, jnp.float32), jnp.zeros(w_out.shape, jnp.float32))
    (grad_w_in, grad_w_out), (layer_out, d_emb) = lax.scan(per_group, start, (embedded, segment, cotangent))
    grad_table = jnp.zeros(table.shape, jnp.float32).at[item_index.reshape(-1)].add(d_emb.reshape(-1, table.shape[1]).astype(jnp.float32))
    return (layer_out, grad_table, grad_w_in, grad_w_out)
```

```python
import jax
import jax.numpy as jnp
from jax import lax
from jax.experimental import pallas as pl
from jax.experimental.pallas import tpu as pltpu
from jax.sharding import Mesh, PartitionSpec as P

HEADS = 8
EPS = 1e-05
CAP = 8
BF = jnp.bfloat16
F32 = jnp.float32
TABLE = ("y", "z")
DP = ("x", "c")
ALL = ("y", "z", "x", "c")


def iota(shape, dim):
    return lax.broadcasted_iota(jnp.int32, shape, dim)


def dot(a, b, dims=((1,), (0,))):
    return lax.dot_general(a, b, (dims, ((), ())), preferred_element_type=F32)


def plan_kernel(owner_ref, row_ref, request_ref, slot_ref):
    rows = owner_ref.shape[1]
    shards = request_ref.shape[0]
    own = owner_ref[...].astype(F32)
    row = row_ref[...].astype(F32)
    first = iota((rows, rows), 0)
    second = iota((rows, rows), 1)
    own_col = jnp.sum(jnp.where(first == second, own, 0.0), axis=1, keepdims=True)
    earlier = (own_col == own) & (first < second)
    rank = jnp.sum(jnp.where(earlier, 1.0, 0.0), axis=0, keepdims=True)
    slot_ref[...] = (own * CAP + rank).astype(jnp.int32)
    mine = jnp.where(iota((shards, rows), 0).astype(F32) == own, row + 1.0, 0.0)
    lane = iota((shards, 128), 1)
    request = jnp.full((shards, 128), -1.0, F32)
    for k in range(CAP):
        found = jnp.sum(jnp.where(rank == float(k), mine, 0.0), axis=1, keepdims=True)
        request = jnp.where(lane == k, found - 1.0, request)
    request_ref[...] = request.astype(jnp.int32)


def plan(owner, row, shards):
    return pl.pallas_call(
        plan_kernel,
        out_shape=(
            jax.ShapeDtypeStruct((shards, 128), jnp.int32),
            jax.ShapeDtypeStruct(owner.shape, jnp.int32),
        ),
        name="plan",
    )(owner, row)


def chosen_rows(asked_ref, vocab_rows):
    shards = asked_ref.shape[0]
    slots = shards * CAP
    asked = asked_ref[...].astype(F32)
    spread = jnp.broadcast_to(asked[:, None, :], (shards, CAP, 128)).reshape(slots, 128)
    keep = iota((slots, 128), 1) == (iota((slots, 128), 0) % CAP)
    column = jnp.sum(jnp.where(keep, spread, 0.0), axis=1, keepdims=True)
    return jnp.where(column == iota((slots, vocab_rows), 1).astype(F32), 1.0, 0.0).astype(BF)


def serve_kernel(asked_ref, table_ref, found_ref):
    found_ref[...] = dot(chosen_rows(asked_ref, table_ref.shape[0]), table_ref[...]).astype(BF)


def serve(asked, table):
    return pl.pallas_call(
        serve_kernel,
        out_shape=jax.ShapeDtypeStruct((asked.shape[0] * CAP, table.shape[1]), BF),
        name="serve",
    )(asked, table)


def collect_kernel(asked_ref, grads_ref, sum_ref):
    chosen = chosen_rows(asked_ref, sum_ref.shape[0])
    sum_ref[...] = dot(chosen, grads_ref[...], ((0,), (0,))).astype(sum_ref.dtype)


def collect(asked, grads, vocab_rows):
    return pl.pallas_call(
        collect_kernel,
        out_shape=jax.ShapeDtypeStruct((vocab_rows, grads.shape[1]), BF),
        name="collect",
    )(asked, grads)


def layer_kernel(
    slot_ref, segment_ref, returned_ref, w_in_ref, w_out_ref, cot_ref,
    out_ref, d_in_ref, d_out_ref, sent_ref,
    mixed, slope, attended, d_mixed,
):
    rows, width = cot_ref.shape
    slots = returned_ref.shape[0]
    head = width // HEADS
    pair = 2 * head
    scale = head ** (-0.5)
    match = jnp.where(iota((slots, rows), 0) == slot_ref[...], 1.0, 0.0).astype(BF)
    embedded = dot(match, returned_ref[...], ((0,), (0,)))
    average = jnp.mean(embedded, axis=-1, keepdims=True)
    centred = embedded - average
    inverse = lax.rsqrt(jnp.mean(centred * centred, axis=-1, keepdims=True) + EPS)
    hat = centred * inverse
    normed = hat.astype(BF)
    for part in range(4):
        span = slice(part * width, (part + 1) * width)
        pre = dot(normed, w_in_ref[:, span])
        sig = jax.nn.sigmoid(pre)
        value = pre * sig
        mixed[:, span] = value.astype(BF)
        slope[:, span] = sig + value * (1.0 - sig)
    seg = segment_ref[...].astype(F32)
    first = iota((rows, rows), 0)
    second = iota((rows, rows), 1)
    seg_col = jnp.sum(jnp.where(first == second, seg, 0.0), axis=1, keepdims=True)
    allowed = (seg_col == seg) & (second <= first)
    low = iota((rows, pair), 1) < head
    zero = jnp.zeros((rows, pair), BF)

    def parts(block):
        return jnp.where(low, block, zero), jnp.where(low, zero, block)

    def at(part, p):
        return slice(part * width + p * pair, part * width + (p + 1) * pair)

    def weigh(q, k):
        score = dot(q, k, ((1,), (1,))) * scale
        sig = jax.nn.sigmoid(score)
        return score, sig

    for p in range(HEADS // 2):
        values, keys = mixed[:, at(1, p)], mixed[:, at(3, p)]
        halves = []
        for q in parts(mixed[:, at(2, p)]):
            score, sig = weigh(q, keys)
            weights = jnp.where(allowed, score * sig, 0.0).astype(BF)
            halves.append(dot(weights, values))
        attended[:, p * pair : (p + 1) * pair] = jnp.where(low, halves[0], halves[1])
    att = attended[...]
    centred = att - jnp.mean(att, axis=-1, keepdims=True)
    inverse_a = lax.rsqrt(jnp.mean(centred * centred, axis=-1, keepdims=True) + EPS)
    hat_a = centred * inverse_a
    gate = mixed[:, :width].astype(F32)
    gated = (hat_a * gate).astype(BF)
    out_ref[...] = (embedded + dot(gated, w_out_ref[...])).astype(BF)
    cot = cot_ref[...]
    d_out_ref[...] = dot(gated, cot, ((0,), (0,))).astype(BF)
    d_gated = dot(cot, w_out_ref[...], ((1,), (1,))).astype(BF).astype(F32)
    d_mixed[:, :width] = ((d_gated * hat_a).astype(BF).astype(F32) * slope[:, :width]).astype(BF)
    d_hat = d_gated * gate
    d_att = inverse_a * (
        d_hat
        - jnp.mean(d_hat, axis=-1, keepdims=True)
        - hat_a * jnp.mean(d_hat * hat_a, axis=-1, keepdims=True)
    )
    attended[...] = d_att
    for p in range(HEADS // 2):
        values, keys, queries = mixed[:, at(1, p)], mixed[:, at(3, p)], mixed[:, at(2, p)]
        d_pair = attended[:, p * pair : (p + 1) * pair].astype(BF)
        found = []
        for q, d_half in zip(parts(queries), parts(d_pair)):
            score, sig = weigh(q, keys)
            value = score * sig
            weights = jnp.where(allowed, value, 0.0).astype(BF)
            d_weights = dot(d_half, values, ((1,), (1,))).astype(BF).astype(F32)
            d_score = jnp.where(
                allowed, d_weights * (sig + value * (1.0 - sig)) * scale, 0.0
            ).astype(BF)
            found.append(
                (
                    dot(weights, d_pair, ((0,), (0,))),
                    dot(d_score, keys),
                    dot(d_score, queries, ((0,), (0,))),
                )
            )
        for part in range(3):
            span = at(part + 1, p)
            whole = jnp.where(low, found[0][part], found[1][part]).astype(BF).astype(F32)
            d_mixed[:, span] = (whole * slope[:, span]).astype(BF)
    d_all = d_mixed[...]
    d_in_ref[...] = dot(normed, d_all, ((0,), (0,))).astype(BF)
    d_normed = dot(d_all, w_in_ref[...], ((1,), (1,))).astype(BF).astype(F32)
    d_emb = inverse * (
        d_normed
        - jnp.mean(d_normed, axis=-1, keepdims=True)
        - hat * jnp.mean(d_normed * hat, axis=-1, keepdims=True)
    )
    d_emb = (cot.astype(F32) + d_emb).astype(BF)
    sent_ref[...] = dot(match, d_emb).astype(BF)


def layer(slot, segment, returned, w_in, w_out, cot):
    rows, width = cot.shape
    return pl.pallas_call(
        layer_kernel,
        out_shape=(
            jax.ShapeDtypeStruct((rows, width), BF),
            jax.ShapeDtypeStruct(w_in.shape, BF),
            jax.ShapeDtypeStruct(w_out.shape, BF),
            jax.ShapeDtypeStruct(returned.shape, BF),
        ),
        scratch_shapes=[
            pltpu.VMEM((rows, 4 * width), BF),
            pltpu.VMEM((rows, 4 * width), F32),
            pltpu.VMEM((rows, width), F32),
            pltpu.VMEM((rows, 4 * width), BF),
        ],
        name="layer",
    )(slot, segment, returned, w_in, w_out, cot)


def share_sum_kernel(own_ref, a_ref, b_ref, c_ref, sum_ref):
    total = own_ref[...].astype(F32) + a_ref[...].astype(F32)
    total = total + b_ref[...].astype(F32) + c_ref[...].astype(F32)
    sum_ref[...] = total.astype(sum_ref.dtype)


def shift(x, axis, by, size):
    return lax.ppermute(x, axis, [(i, (i + by) % size) for i in range(size)])


def exchange(x, axes):
    return lax.all_to_all(x, axes, split_axis=0, concat_axis=0, tiled=True)


def part_of(x, index):
    return lax.dynamic_index_in_dim(x, index, 0, keepdims=False)


def on_device(table, owner, row_in_shard, segment, w_in, w_out, cotangent):
    shards = 64
    vocab_rows, width = table.shape
    rows = owner.shape[1]
    x, c = lax.axis_index("x"), lax.axis_index("c")
    request, slot = plan(owner.reshape(1, rows), row_in_shard, shards)
    asked = exchange(request.reshape(shards, 1, 128), TABLE).reshape(shards, 128)
    found = serve(asked, table)
    returned = exchange(found.reshape(shards, CAP, width), TABLE).reshape(shards * CAP, width)
    out, d_in, d_out, sent = layer(slot, segment, returned, w_in, w_out, cotangent[0])
    blocks = jnp.concatenate(
        [
            d_in.reshape(width, 4, 2, 256).transpose(1, 2, 0, 3).reshape(4, 2, 256, 512),
            d_out.reshape(4, 2, 64, 512),
        ],
        axis=2,
    )
    mine = lax.dynamic_index_in_dim(blocks, c, 1, keepdims=False)
    other = lax.dynamic_index_in_dim(blocks, 1 - c, 1, keepdims=False)
    other = lax.ppermute(other, "c", [(0, 1), (1, 0)])
    halves = (mine.astype(F32) + other.astype(F32)).astype(BF)
    arrived = exchange(sent.reshape(shards, CAP, width), TABLE).reshape(shards * CAP, width)
    pieces = [part_of(halves, x)] + [
        shift(part_of(halves, (x + k) % 4), "x", k, 4) for k in (1, 2, 3)
    ]
    share = sum(p.astype(F32) for p in pieces)
    share = exchange(share.astype(BF).reshape(shards, 2560), TABLE)
    share = jnp.sum(share.astype(F32), axis=0).astype(BF)
    share = exchange(jnp.broadcast_to(share[None], (shards, 2560)), TABLE).astype(F32)
    share = share.reshape(320, 512)
    part = collect(asked, arrived, vocab_rows)
    part = part.reshape(2, 192, width)
    other = lax.ppermute(part_of(part, 1 - c), "c", [(0, 1), (1, 0)])
    half = (part_of(part, c).astype(F32) + other.astype(F32)).astype(BF)
    halves = [half] + [shift(half, "x", k, 4) for k in (1, 2, 3)]
    half = sum(h.astype(F32) for h in halves)
    other = lax.ppermute(half, "c", [(0, 1), (1, 0)])
    grad_table = jnp.where(c == 0, jnp.concatenate([half, other]), jnp.concatenate([other, half]))
    return out[None], grad_table, share[:256].reshape(512, 256), share[256:]


def solution(mesh):
    devices = mesh.devices
    grid = Mesh(devices.reshape(4, 16, 4, 2), ALL)
    placed = (
        P(TABLE, None),
        P(ALL, None, None),
        P(ALL, None),
        P(ALL, None),
        P(),
        P(),
        P(ALL, None, None),
    )
    return jax.shard_map(
        on_device,
        mesh=grid,
        in_specs=placed,
        out_specs=(P(ALL, None, None), P(TABLE, None), P(None, DP), P(DP, None)),
        check_vma=False,
    )
```

```python
import jax
import jax.numpy as jnp
from jax import lax
from jax.experimental import pallas as pl
from jax.experimental.pallas import tpu as pltpu
from jax.sharding import Mesh, PartitionSpec as P

HEADS = 8
EPS = 1e-05
CAP = 8
Y, Z, X = 4, 16, 4
PIECE = 20
BF = jnp.bfloat16
F32 = jnp.float32
TABLE = ("y", "z")
DP = ("x", "c")
ALL = ("y", "z", "x", "c")


def iota(shape, dim):
    return lax.broadcasted_iota(jnp.int32, shape, dim)


def dot(a, b, dims=((1,), (0,))):
    return lax.dot_general(a, b, (dims, ((), ())), preferred_element_type=F32)


def plan_kernel(owner_ref, row_ref, request_ref, slot_ref):
    rows = owner_ref.shape[1]
    shards = request_ref.shape[0]
    own = owner_ref[...].astype(F32)
    row = row_ref[...].astype(F32)
    first = iota((rows, rows), 0)
    second = iota((rows, rows), 1)
    own_col = jnp.sum(jnp.where(first == second, own, 0.0), axis=1, keepdims=True)
    earlier = (own_col == own) & (first < second)
    rank = jnp.sum(jnp.where(earlier, 1.0, 0.0), axis=0, keepdims=True)
    slot_ref[...] = (own * CAP + rank).astype(jnp.int32)
    mine = jnp.where(iota((shards, rows), 0).astype(F32) == own, row + 1.0, 0.0)
    lane = iota((shards, 128), 1)
    request = jnp.full((shards, 128), -1.0, F32)
    for k in range(CAP):
        found = jnp.sum(jnp.where(rank == float(k), mine, 0.0), axis=1, keepdims=True)
        request = jnp.where(lane == k, found - 1.0, request)
    request_ref[...] = request.astype(jnp.int32)


def plan(owner, row, shards):
    return pl.pallas_call(
        plan_kernel,
        out_shape=(
            jax.ShapeDtypeStruct((shards, 128), jnp.int32),
            jax.ShapeDtypeStruct(owner.shape, jnp.int32),
        ),
        name="plan",
    )(owner, row)


def chosen_rows(asked_ref, vocab_rows):
    shards = asked_ref.shape[0]
    slots = shards * CAP
    asked = asked_ref[...].astype(F32)
    spread = jnp.broadcast_to(asked[:, None, :], (shards, CAP, 128)).reshape(slots, 128)
    keep = iota((slots, 128), 1) == (iota((slots, 128), 0) % CAP)
    column = jnp.sum(jnp.where(keep, spread, 0.0), axis=1, keepdims=True)
    return jnp.where(column == iota((slots, vocab_rows), 1).astype(F32), 1.0, 0.0).astype(BF)


def serve_kernel(asked_ref, table_ref, found_ref):
    found_ref[...] = dot(chosen_rows(asked_ref, table_ref.shape[0]), table_ref[...]).astype(BF)


def serve(asked, table):
    return pl.pallas_call(
        serve_kernel,
        out_shape=jax.ShapeDtypeStruct((asked.shape[0] * CAP, table.shape[1]), BF),
        name="serve",
    )(asked, table)


def collect_kernel(asked_ref, grads_ref, mine_ref, other_ref, total):
    half = mine_ref.shape[0]
    chosen = chosen_rows(asked_ref, 2 * half)
    total[...] = dot(chosen, grads_ref[...], ((0,), (0,)))
    core = lax.axis_index("c")
    for half_ref, c in ((mine_ref, core), (other_ref, 1 - core)):
        half_ref[...] = total[pl.ds(pl.multiple_of(c * half, half), half), :].astype(BF)


def collect(asked, grads, vocab_rows):
    half = jax.ShapeDtypeStruct((vocab_rows // 2, grads.shape[1]), BF)
    return pl.pallas_call(
        collect_kernel,
        out_shape=(half, half),
        scratch_shapes=[pltpu.VMEM((vocab_rows, grads.shape[1]), F32)],
        name="collect",
    )(asked, grads)


def place_kernel(mine_ref, other_ref, whole_ref):
    half = mine_ref.shape[0]
    core = lax.axis_index("c")
    whole_ref[pl.ds(pl.multiple_of(core * half, half), half), :] = mine_ref[...]
    whole_ref[pl.ds(pl.multiple_of((1 - core) * half, half), half), :] = other_ref[...]


def place(mine, other):
    return pl.pallas_call(
        place_kernel,
        out_shape=jax.ShapeDtypeStruct((2 * mine.shape[0], mine.shape[1]), F32),
        name="place",
    )(mine, other)


def split_kernel(arrived_ref, pieces_ref):
    _, size, _ = arrived_ref.shape
    total = jnp.sum(arrived_ref[...].astype(F32), axis=0)
    for z in range(size // PIECE):
        pieces_ref[z] = total[z * PIECE : (z + 1) * PIECE].astype(BF)


def split(arrived):
    _, size, lanes = arrived.shape
    return pl.pallas_call(
        split_kernel,
        out_shape=jax.ShapeDtypeStruct((size // PIECE, PIECE, lanes), BF),
        name="split",
    )(arrived)


def spread_kernel(arrived_ref, copies_ref):
    total = jnp.sum(arrived_ref[...].astype(F32), axis=0).astype(BF)
    copies_ref[...] = jnp.broadcast_to(total[None], copies_ref.shape)


def spread(arrived, copies):
    return pl.pallas_call(
        spread_kernel,
        out_shape=jax.ShapeDtypeStruct((copies,) + arrived.shape[1:], BF),
        name="spread",
    )(arrived)


def finish_kernel(pieces_ref, in_ref, out_ref):
    flat = jnp.concatenate([pieces_ref[k].astype(F32) for k in range(pieces_ref.shape[0])], axis=0)
    in_ref[:, :128] = flat[:512]
    in_ref[:, 128:] = flat[512:1024]
    for j in range(4):
        out_ref[:, 128 * j : 128 * (j + 1)] = flat[1024 + 64 * j : 1088 + 64 * j]


def finish(pieces):
    return pl.pallas_call(
        finish_kernel,
        out_shape=(
            jax.ShapeDtypeStruct((512, 256), F32),
            jax.ShapeDtypeStruct((64, 512), F32),
        ),
        name="finish",
    )(pieces)


def layer_kernel(
    slot_ref, segment_ref, returned_ref, w_in_ref, w_out_ref, cot_ref,
    out_ref, sent_ref, mine_ref, other_ref,
    mixed, slope, attended, d_mixed, d_out,
):
    rows, width = cot_ref.shape
    slots = returned_ref.shape[0]
    head = width // HEADS
    pair = 2 * head
    scale = head ** (-0.5)
    match = jnp.where(iota((slots, rows), 0) == slot_ref[...], 1.0, 0.0).astype(BF)
    embedded = dot(match, returned_ref[...], ((0,), (0,)))
    average = jnp.mean(embedded, axis=-1, keepdims=True)
    centred = embedded - average
    inverse = lax.rsqrt(jnp.mean(centred * centred, axis=-1, keepdims=True) + EPS)
    hat = centred * inverse
    normed = hat.astype(BF)
    for part in range(4):
        span = slice(part * width, (part + 1) * width)
        pre = dot(normed, w_in_ref[:, span])
        sig = jax.nn.sigmoid(pre)
        value = pre * sig
        mixed[:, span] = value.astype(BF)
        slope[:, span] = sig + value * (1.0 - sig)
    seg = segment_ref[...].astype(F32)
    first = iota((rows, rows), 0)
    second = iota((rows, rows), 1)
    seg_col = jnp.sum(jnp.where(first == second, seg, 0.0), axis=1, keepdims=True)
    allowed = (seg_col == seg) & (second <= first)
    low = iota((rows, pair), 1) < head
    zero = jnp.zeros((rows, pair), BF)

    def parts(block):
        return jnp.where(low, block, zero), jnp.where(low, zero, block)

    def at(part, p):
        return slice(part * width + p * pair, part * width + (p + 1) * pair)

    def weigh(q, k):
        score = dot(q, k, ((1,), (1,))) * scale
        sig = jax.nn.sigmoid(score)
        return score, sig

    for p in range(HEADS // 2):
        values, keys = mixed[:, at(1, p)], mixed[:, at(3, p)]
        halves = []
        for q in parts(mixed[:, at(2, p)]):
            score, sig = weigh(q, keys)
            weights = jnp.where(allowed, score * sig, 0.0).astype(BF)
            halves.append(dot(weights, values))
        attended[:, p * pair : (p + 1) * pair] = jnp.where(low, halves[0], halves[1])
    att = attended[...]
    centred = att - jnp.mean(att, axis=-1, keepdims=True)
    inverse_a = lax.rsqrt(jnp.mean(centred * centred, axis=-1, keepdims=True) + EPS)
    hat_a = centred * inverse_a
    gate = mixed[:, :width].astype(F32)
    gated = (hat_a * gate).astype(BF)
    out_ref[...] = (embedded + dot(gated, w_out_ref[...])).astype(BF)
    cot = cot_ref[...]
    d_out[...] = dot(gated, cot, ((0,), (0,)))
    d_gated = dot(cot, w_out_ref[...], ((1,), (1,))).astype(BF).astype(F32)
    d_mixed[:, :width] = ((d_gated * hat_a).astype(BF).astype(F32) * slope[:, :width]).astype(BF)
    d_hat = d_gated * gate
    d_att = inverse_a * (
        d_hat
        - jnp.mean(d_hat, axis=-1, keepdims=True)
        - hat_a * jnp.mean(d_hat * hat_a, axis=-1, keepdims=True)
    )
    attended[...] = d_att
    for p in range(HEADS // 2):
        values, keys, queries = mixed[:, at(1, p)], mixed[:, at(3, p)], mixed[:, at(2, p)]
        d_pair = attended[:, p * pair : (p + 1) * pair].astype(BF)
        found = []
        for q, d_half in zip(parts(queries), parts(d_pair)):
            score, sig = weigh(q, keys)
            value = score * sig
            weights = jnp.where(allowed, value, 0.0).astype(BF)
            d_weights = dot(d_half, values, ((1,), (1,))).astype(BF).astype(F32)
            d_score = jnp.where(
                allowed, d_weights * (sig + value * (1.0 - sig)) * scale, 0.0
            ).astype(BF)
            found.append(
                (
                    dot(weights, d_pair, ((0,), (0,))),
                    dot(d_score, keys),
                    dot(d_score, queries, ((0,), (0,))),
                )
            )
        for part in range(3):
            span = at(part + 1, p)
            whole = jnp.where(low, found[0][part], found[1][part]).astype(BF).astype(F32)
            d_mixed[:, span] = (whole * slope[:, span]).astype(BF)
    d_all = d_mixed[...]
    d_normed = dot(d_all, w_in_ref[...], ((1,), (1,))).astype(BF).astype(F32)
    d_emb = inverse * (
        d_normed
        - jnp.mean(d_normed, axis=-1, keepdims=True)
        - hat * jnp.mean(d_normed * hat, axis=-1, keepdims=True)
    )
    d_emb = (cot.astype(F32) + d_emb).astype(BF)
    sent_ref[...] = dot(match, d_emb).astype(BF)
    core = lax.axis_index("c")
    for block_ref, c in ((mine_ref, core), (other_ref, 1 - core)):
        for k in range(X):
            d = 2 * k + c
            columns = pl.ds(pl.multiple_of(d * 256, 256), 256)
            d_in = dot(normed, d_mixed[:, columns], ((0,), (0,))).astype(BF)
            d_rows = d_out[pl.ds(pl.multiple_of(d * 64, 64), 64), :].astype(BF)
            parts_of = [d_in[:, :128], d_in[:, 128:]]
            parts_of += [d_rows[:, 128 * j : 128 * (j + 1)] for j in range(4)]
            block = jnp.concatenate(parts_of, axis=0)
            for y in range(Y):
                block_ref[y, k] = block[y * 320 : (y + 1) * 320]


def layer(slot, segment, returned, w_in, w_out, cot):
    rows, width = cot.shape
    return pl.pallas_call(
        layer_kernel,
        out_shape=(
            jax.ShapeDtypeStruct((rows, width), BF),
            jax.ShapeDtypeStruct(returned.shape, BF),
            jax.ShapeDtypeStruct((Y, X, 320, 128), BF),
            jax.ShapeDtypeStruct((Y, X, 320, 128), BF),
        ),
        scratch_shapes=[
            pltpu.VMEM((rows, 4 * width), BF),
            pltpu.VMEM((rows, 4 * width), F32),
            pltpu.VMEM((rows, width), F32),
            pltpu.VMEM((rows, 4 * width), BF),
            pltpu.VMEM((width, width), F32),
        ],
        name="layer",
    )(slot, segment, returned, w_in, w_out, cot)


def exchange(x, axes):
    return lax.all_to_all(x, axes, split_axis=0, concat_axis=0, tiled=True)


def on_device(table, owner, row_in_shard, segment, w_in, w_out, cotangent):
    shards = Y * Z
    vocab_rows, width = table.shape
    rows = owner.shape[1]
    request, slot = plan(owner.reshape(1, rows), row_in_shard, shards)
    asked = exchange(request.reshape(shards, 1, 128), TABLE).reshape(shards, 128)
    found = serve(asked, table)
    returned = exchange(found.reshape(shards, CAP, width), TABLE).reshape(shards * CAP, width)
    out, sent, mine, other = layer(slot, segment, returned, w_in, w_out, cotangent[0])
    other = lax.ppermute(other, "c", [(0, 1), (1, 0)])
    arrived = exchange(sent.reshape(shards, CAP, width), TABLE)
    arrived = arrived.reshape(shards * CAP, width)
    halves = (mine.astype(F32) + other.astype(F32)).astype(BF)
    share = exchange(halves.reshape(Y * X, 320, 128), ("y", "x"))
    share = exchange(split(share), "z")
    share = exchange(spread(share, shards), TABLE)
    grad_in, grad_out = finish(share)
    mine, other = collect(asked, arrived, vocab_rows)
    other = lax.ppermute(other, "c", [(0, 1), (1, 0)])
    mine = (mine.astype(F32) + other.astype(F32)).astype(BF)
    other = lax.ppermute(mine, "x", [(0, 3), (1, 2), (2, 1), (3, 0)])
    mine = (mine.astype(F32) + other.astype(F32)).astype(BF)
    other = lax.ppermute(mine, "x", [(0, 1), (1, 0), (2, 3), (3, 2)])
    mine = mine.astype(F32) + other.astype(F32)
    other = lax.ppermute(mine, "c", [(0, 1), (1, 0)])
    grad_table = place(mine, other)
    return out[None], grad_table, grad_in, grad_out


def solution(mesh):
    grid = Mesh(mesh.devices.reshape(Y, Z, X, 2), ALL)
    placed = (
        P(TABLE, None),
        P(ALL, None, None),
        P(ALL, None),
        P(ALL, None),
        P(),
        P(),
        P(ALL, None, None),
    )
    return jax.shard_map(
        on_device,
        mesh=grid,
        in_specs=placed,
        out_specs=(P(ALL, None, None), P(TABLE, None), P(None, DP), P(DP, None)),
        check_vma=False,
    )
```
